256 devices in a mesh: gx: 8 (over z_lo, y), gy: 4 (over x), gz: 8 (over z_hi, core).
Axes of the slice: x: 4, y: 4, z: 8 (z_hi: 4, z_lo: 2; z = z_hi * 2 + z_lo), core: 2. Of those that a mesh axis runs over, the one named last changes fastest.
Arguments:
- volume: bfloat16 [128, 64, 64, 256], P('gx', 'gy', 'gz'), may hold values from -6 to 6
- offsets: int32 [2, 3], replicated, may hold values from 0 to 4, as said below
- coefficients: float32 [5], replicated, may hold values from -0.15 to 0.5
Outputs:
- denoised: bfloat16 [128, 64, 64, 256], P('gx', 'gy', 'gz')
The draws below stay inside these ranges and needn't reach their ends.
Inputs may be any that keep to these rules, and one draw needn't show every extreme that they name: `offsets`: every entry is 0 or 4; along each spatial dimension at least one of the passes has 4.
All inputs are finite; a program needn't handle non-finite values.
Results may differ from the reference program's by a relative error of at most 0.0062.
Values may be sent and summed in bfloat16 or wider, within the bound.
A program may use at most 64 MiB of HBM per device.

```python
import jax
import jax.numpy as jnp
from jax import lax

FRAMES = 256
BLK = 8
PASSES = 2
SHIFT = 4
VOXB = 512
NX = 128
NY = 64
NZ = 64


def draw_offsets(key, part):
    pattern = jax.random.randint(key, (3,), 0, 3)
    leading = jnp.where(pattern != 1, SHIFT, 0)
    trailing = jnp.where(pattern != 0, SHIFT, 0)
    return jnp.stack([leading, trailing]).astype(jnp.int32)


def draw_coefficients(key, part):
    lower_end = jnp.array([0.2, 0.3, -0.15, 0.01, -0.004], jnp.float32)
    upper_end = jnp.array([0.4, 0.5, -0.05, 0.04, -0.001], jnp.float32)
    uniform_draw = jax.random.uniform(key, (5,), jnp.float32)
    return (lower_end + (upper_end - lower_end) * uniform_draw).astype(jnp.float32)


def shard_levels(rng, shape, cuts, low, largest):
    gain = 1.0
    for axis_at, blocks in cuts:
        draws = jax.random.uniform(jax.random.fold_in(jax.random.fold_in(rng, 6), axis_at), (blocks,), jnp.float32, low / len(cuts), largest / len(cuts))
        gain = gain * jnp.repeat(jnp.exp(draws), shape[axis_at] // blocks).reshape((-1,) + (1,) * (len(shape) - 1 - axis_at))
    return gain


def scatter_about(key, dims, spread, bound, shards=(), kind=jnp.bfloat16):
    entries = spread * jax.random.normal(key, dims, jnp.float32)
    if shards:
        entries = entries * shard_levels(key, dims, shards, -0.22, 0.18)
    return jnp.clip(entries, -bound, bound).astype(kind)


def setup_inputs(seed: int = 0) -> dict:
    key_list = jax.random.split(jax.random.key(seed), 4)
    volume = scatter_about(key_list[0], (NX, NY, NZ, FRAMES), 1.0, 6.0, ((0, 8), (1, 4), (2, 8)))
    offsets = draw_offsets(jax.random.fold_in(key_list[3], 71), 0)
    coefficients = draw_coefficients(jax.random.fold_in(key_list[3], 71), 0)
    return dict(volume=volume, offsets=offsets, coefficients=coefficients)


def to_blocks(volume_now):
    sizes = volume_now.shape
    shaped = volume_now.reshape(sizes[0] // BLK, BLK, sizes[1] // BLK, BLK, sizes[2] // BLK, BLK, sizes[3])
    return shaped.transpose(0, 2, 4, 1, 3, 5, 6).reshape(-1, VOXB, sizes[3])


def from_blocks(blocks, sizes):
    shaped = blocks.reshape(sizes[0] // BLK, sizes[1] // BLK, sizes[2] // BLK, BLK, BLK, BLK, sizes[3])
    return shaped.transpose(0, 3, 1, 4, 2, 5, 6).reshape(sizes)


def shrink(blocks, coefficients):
    highest = lax.Precision.HIGHEST
    wide = blocks.astype(jnp.float32)
    gramian = jnp.einsum('bvf,bvg->bfg', wide, wide, precision=highest)
    frames = gramian.shape[-1]
    voxels = blocks.shape[1]
    diag_mean = jnp.trace(gramian, axis1=1, axis2=2) / (voxels * frames)
    scaled = gramian / (voxels * (diag_mean + 1e-6))[:, None, None]
    identity = jnp.eye(frames, dtype=jnp.float32)
    poly = coefficients[4] * scaled + coefficients[3] * identity
    for degree_index in (2, 1, 0):
        poly = jnp.einsum('bfg,bgh->bfh', poly, scaled, precision=highest) + coefficients[degree_index] * identity
    poly_half = poly.astype(jnp.bfloat16).astype(jnp.float32)
    result = jnp.einsum('bvf,bfg->bvg', wide, poly_half, precision=highest)
    return result.astype(jnp.bfloat16)


def one_pass(volume_now, shifts, coefficients):
    rolled = volume_now
    for axis_index in range(3):
        rolled = jnp.roll(rolled, -shifts[axis_index], axis=axis_index)
    blocks = to_blocks(rolled)
    groups = blocks.reshape(-1, 16, VOXB, blocks.shape[2])
    finished = lax.map(lambda group: shrink(group, coefficients), groups)
    shrunk = from_blocks(finished.reshape(blocks.shape), rolled.shape)
    for axis_index in range(3):
        shrunk = jnp.roll(shrunk, shifts[axis_index], axis=axis_index)
    return shrunk


def reference(volume, offsets, coefficients):
    current = volume
    for pass_index in range(PASSES):
        current = one_pass(current, offsets[pass_index], coefficients)
    return current
```

```python
import functools

import jax
import jax.numpy as jnp
from jax import lax
from jax.experimental import pallas as pl
from jax.experimental.pallas import tpu as pltpu
from jax.sharding import PartitionSpec as P

SLOTS = [(a, b, c) for a in range(4) for b in range(4) for c in range(2)]
ROWS = 64
CUBE = 512
FRAMES = 256
AXES = ("gx", "gy", "gz")

OWNERS = [
    ((1, 0, 3), (0, 0, 0)), ((1, 1, 0), (0, 0, 3)), ((1, 0, 5), (0, 0, 3)),
    ((1, 0, 3), (0, 1, 0)), ((1, 0, 0), (0, 1, 3)), ((1, 0, 5), (0, 1, 3)),
    ((1, 0, 3), (0, 1, 0)), ((1, 1, 0), (0, 1, 3)), ((1, 0, 5), (0, 0, 5)),
    ((0, 1, 3), (1, 0, 0)), ((0, 1, 0), (1, 0, 3)), ((0, 1, 3), (1, 0, 5)),
    ((0, 0, 3), (1, 1, 0)), ((0, 0, 0), (1, 0, 3)), ((0, 0, 3), (1, 0, 5)),
    ((0, 0, 3), (1, 2, 0)), ((0, 1, 0), (1, 0, 3)), ((0, 0, 5), (1, 0, 5)),
    ((1, 0, 3), (1, 0, 0)), ((1, 1, 0), (1, 0, 3)), ((1, 1, 3), (1, 0, 3)),
    ((1, 0, 3), (1, 1, 0)), ((1, 0, 0), (1, 0, 3)), ((1, 0, 3), (1, 1, 3)),
    ((1, 1, 3), (1, 1, 0)), ((1, 1, 0), (1, 1, 3)), ((1, 0, 3), (1, 0, 3)),
]


def place(index, moved, count):
    if not moved:
        return index // 2, index % 2, False
    turned = (index - 1) % count
    return turned // 2, turned % 2, turned // 2 == count // 2 - 1


def layout(moved, owners):
    rows = []
    for a, b, c in SLOTS:
        i, px, sx = place(a, moved[0], 4)
        j, py, sy = place(b, moved[1], 4)
        _, pz, sz = place(c, moved[2], 2)
        step = (
            (owners[0] >> j & 1) - px if sx else 0,
            (owners[1] >> i & 1) - py if sy else 0,
            (owners[2] >> (2 * i + j) & 1) - pz if sz else 0,
        )
        rows.append((2 * i + j, (px * 2 + py) * 2 + pz, step))
    return rows


def minus(left, right):
    return tuple(x - y for x, y in zip(left, right))


def shrink_cube(cube, coefficients, diagonal):
    c0, c1, c2, c3, c4 = coefficients

    def product(left, right):
        return lax.dot_general(
            left, right, (((1,), (0,)), ((), ())), preferred_element_type=jnp.float32
        )

    def halves(value):
        high = value.astype(jnp.bfloat16)
        return high, (value - high.astype(jnp.float32)).astype(jnp.bfloat16)

    gramian = lax.dot_general(
        cube, cube, (((0,), (0,)), ((), ())), preferred_element_type=jnp.float32
    )
    trace = jnp.sum(jnp.where(diagonal, gramian, 0.0), keepdims=True)
    scaled = gramian * (1.0 / (CUBE * (trace / (CUBE * FRAMES) + 1e-6)))
    s_high, s_low = halves(scaled)
    square = product(s_high, s_high) + (product(s_high, s_low) + product(s_low, s_high))
    t_high, t_low = halves(square)
    inner = c4 * square + c3 * scaled + jnp.where(diagonal, c2, 0.0)
    q_high, q_low = halves(inner)
    poly = product(q_high, t_high) + (product(q_high, t_low) + product(q_low, t_high))
    poly = poly + c1 * scaled + jnp.where(diagonal, c0, 0.0)
    return product(cube, poly.astype(jnp.bfloat16)).astype(jnp.bfloat16)


def kernel(plan, counts, coef_ref, x_ref, o_ref, in0, out0, in1, out1, sent, came):
    first, second = plan
    stages = (
        [row[2] for row in first],
        [minus(after[2], before[2]) for before, after in zip(first, second)],
        [minus((0, 0, 0), row[2]) for row in second],
    )
    me = [lax.axis_index(axis) for axis in AXES]

    def device(step):
        return tuple(
            lax.rem(here + (s + n), n) if s else here
            for here, s, n in zip(me, step, counts)
        )

    def part(ref, cube, piece):
        return ref.at[cube, pl.ds(ROWS * piece, ROWS)]

    def copy(stage, slot):
        a, b, c = SLOTS[slot]
        k0, q0, _ = first[slot]
        k1, q1, _ = second[slot]
        source = (x_ref.at[a, b, c], part(out0, k0, q0), part(out1, k1, q1))[stage]
        target = (part(in0, k0, q0), part(in1, k1, q1), o_ref.at[a, b, c])[stage]
        step = stages[stage][slot]
        if any(step):
            return pltpu.make_async_remote_copy(
                src_ref=source,
                dst_ref=target,
                send_sem=sent.at[stage, slot],
                recv_sem=came.at[stage, slot],
                device_id=device(step),
                device_id_type=pl.DeviceIdType.MESH,
            ), True
        return pltpu.make_async_copy(source, target, came.at[stage, slot]), False

    def start(stage, slot):
        copy(stage, slot)[0].start()

    def arrive(stage, slot):
        description, remote = copy(stage, slot)
        if remote:
            description.wait_recv()
        else:
            description.wait()

    peers = sorted({step for steps in stages for step in steps if any(step)})
    barrier = pltpu.get_barrier_semaphore()
    for step in peers:
        pl.semaphore_signal(
            barrier,
            inc=1,
            device_id=device(minus((0, 0, 0), step)),
            device_id_type=pl.DeviceIdType.MESH,
        )
    by_cube = lambda rows: sorted(range(32), key=lambda s: (rows[s][0], rows[s][1]))
    for slot in by_cube(first):
        if not any(stages[0][slot]):
            start(0, slot)
    pl.semaphore_wait(barrier, len(peers))
    for slot in by_cube(first):
        if any(stages[0][slot]):
            start(0, slot)

    coefficients = [coef_ref[n] for n in range(5)]
    diagonal = lax.broadcasted_iota(jnp.int32, (FRAMES, FRAMES), 0) == lax.broadcasted_iota(
        jnp.int32, (FRAMES, FRAMES), 1
    )

    for stage, (rows, source, result) in enumerate(((first, in0, out0), (second, in1, out1))):
        mine = lambda cube, rows=rows: [s for s in by_cube(rows) if rows[s][0] == cube]

        def one(k, carry, stage=stage, source=source, result=result, mine=mine):
            for cube in range(4):
                @pl.when(k == cube)
                def _(cube=cube):
                    for slot in mine(cube):
                        arrive(stage, slot)
            result[k] = shrink_cube(source[k], coefficients, diagonal)
            for cube in range(4):
                @pl.when(k == cube)
                def _(cube=cube):
                    for slot in mine(cube):
                        start(stage + 1, slot)
            return carry

        lax.fori_loop(0, 4, one, 0)

    for slot in range(32):
        arrive(2, slot)
    for stage in range(3):
        for slot in range(32):
            if any(stages[stage][slot]):
                copy(stage, slot)[0].wait_send()


def denoise(pattern, counts, coefficients, pieces):
    kinds = (pattern // 9, pattern // 3 % 3, pattern % 3)
    plan = (
        layout([kind != 1 for kind in kinds], OWNERS[pattern][0]),
        layout([kind != 0 for kind in kinds], OWNERS[pattern][1]),
    )
    cubes = pltpu.VMEM((4, CUBE, FRAMES), jnp.bfloat16)
    return pl.pallas_call(
        functools.partial(kernel, plan, counts),
        out_shape=jax.ShapeDtypeStruct(pieces.shape, pieces.dtype),
        in_specs=[
            pl.BlockSpec(memory_space=pltpu.SMEM),
            pl.BlockSpec(memory_space=pl.ANY),
        ],
        out_specs=pl.BlockSpec(memory_space=pl.ANY),
        scratch_shapes=[
            cubes, cubes, cubes, cubes,
            pltpu.SemaphoreType.DMA((3, 32)),
            pltpu.SemaphoreType.DMA((3, 32)),
        ],
        compiler_params=pltpu.CompilerParams(
            collective_id=pattern, has_side_effects=True, vmem_limit_bytes=32 << 20
        ),
        name=f"denoise_{pattern}",
    )(coefficients, pieces)


def local(counts, volume, offsets, coefficients):
    sizes = volume.shape
    pieces = volume.reshape(4, 4, 4, 4, 2, 4, FRAMES).transpose(0, 2, 4, 1, 3, 5, 6)
    pieces = pieces.reshape(4, 4, 2, ROWS, FRAMES)
    kind = jnp.where(offsets[1] != 0, 1 + (offsets[0] != 0).astype(jnp.int32), 0)
    pattern = kind[0] * 9 + kind[1] * 3 + kind[2]
    branches = [functools.partial(denoise, n, counts) for n in range(27)]
    result = lax.switch(pattern, branches, coefficients, pieces)
    result = result.reshape(4, 4, 2, 4, 4, 4, FRAMES).transpose(0, 3, 1, 4, 2, 5, 6)
    return result.reshape(sizes)


def solution(mesh):
    counts = tuple(mesh.shape[axis] for axis in AXES)
    return jax.shard_map(
        functools.partial(local, counts),
        mesh=mesh,
        in_specs=(P("gx", "gy", "gz", None), P(), P()),
        out_specs=P("gx", "gy", "gz", None),
        check_vma=False,
    )
```

```python
import functools

import jax
import jax.numpy as jnp
from jax import lax
from jax.experimental import pallas as pl
from jax.experimental.pallas import tpu as pltpu
from jax.sharding import PartitionSpec as P

ROWS = 64
CUBE = 512
FRAMES = 256
AXES = ("gx", "gy", "gz")

OWNERS = [
    ((1, 0, 3), (0, 0, 0)), ((1, 1, 0), (0, 0, 3)), ((1, 0, 5), (0, 0, 3)),
    ((1, 0, 3), (0, 1, 0)), ((1, 0, 0), (0, 1, 3)), ((1, 0, 5), (0, 1, 3)),
    ((1, 0, 3), (0, 1, 0)), ((1, 1, 0), (0, 1, 3)), ((1, 0, 5), (0, 0, 5)),
    ((0, 1, 3), (1, 0, 0)), ((0, 1, 0), (1, 0, 3)), ((0, 1, 3), (1, 0, 5)),
    ((0, 0, 3), (1, 1, 0)), ((0, 0, 0), (1, 0, 3)), ((0, 0, 3), (1, 0, 5)),
    ((0, 0, 3), (1, 2, 0)), ((0, 1, 0), (1, 0, 3)), ((0, 0, 5), (1, 0, 5)),
    ((1, 0, 3), (1, 0, 0)), ((1, 1, 0), (1, 0, 3)), ((1, 1, 3), (1, 0, 3)),
    ((1, 0, 3), (1, 1, 0)), ((1, 0, 0), (1, 0, 3)), ((1, 0, 3), (1, 1, 3)),
    ((1, 1, 3), (1, 1, 0)), ((1, 1, 0), (1, 1, 3)), ((1, 0, 3), (1, 0, 3)),
]


def grid(moved, owners):
    x_bits = (owners[0] % 2, owners[0] // 2)
    y_bits = (owners[1] % 2, owners[1] // 2)
    z_bits = [owners[2] // 2**n % 2 for n in range(4)]

    def slot_of(cube, piece):
        a = cube // 2 * 2 + piece // 4
        b = cube % 2 * 2 + piece // 2 % 2
        c = piece % 2
        a = (a + 1) % 4 if moved[0] else a
        b = (b + 1) % 4 if moved[1] else b
        return a, b, 1 - c if moved[2] else c

    def cube_of(a, b, c):
        a = (a + 3) % 4 if moved[0] else a
        b = (b + 3) % 4 if moved[1] else b
        c = 1 - c if moved[2] else c
        return a // 2 * 2 + b // 2, a % 2 * 4 + b % 2 * 2 + c

    def step_of(cube, piece):
        i, j = cube // 2, cube % 2
        x = i * (x_bits[0] + j * (x_bits[1] - x_bits[0]) - piece // 4) if moved[0] else 0
        y = j * (y_bits[0] + i * (y_bits[1] - y_bits[0]) - piece // 2 % 2) if moved[1] else 0
        z = 0
        if moved[2]:
            z = z_bits[0] + j * (z_bits[1] - z_bits[0]) + i * (z_bits[2] - z_bits[0])
            z = z + i * j * (z_bits[3] - z_bits[2] - z_bits[1] + z_bits[0]) - piece % 2
        return x, y, z

    return slot_of, cube_of, step_of


def flat(slot):
    return slot[0] * 8 + slot[1] * 2 + slot[2]


def minus(left, right):
    return tuple(x - y for x, y in zip(left, right))


def shrink_cube(cube, coefficients, diagonal):
    c0, c1, c2, c3, c4 = coefficients

    def product(left, right):
        return lax.dot_general(
            left, right, (((1,), (0,)), ((), ())), preferred_element_type=jnp.float32
        )

    def halves(value):
        high = value.astype(jnp.bfloat16)
        return high, (value - high.astype(jnp.float32)).astype(jnp.bfloat16)

    gramian = lax.dot_general(
        cube, cube, (((0,), (0,)), ((), ())), preferred_element_type=jnp.float32
    )
    trace = jnp.sum(jnp.where(diagonal, gramian, 0.0), keepdims=True)
    scaled = gramian * (1.0 / (CUBE * (trace / (CUBE * FRAMES) + 1e-6)))
    s_high, s_low = halves(scaled)
    square = product(s_high, s_high) + (product(s_high, s_low) + product(s_low, s_high))
    t_high, t_low = halves(square)
    inner = c4 * square + c3 * scaled + jnp.where(diagonal, c2, 0.0)
    q_high, q_low = halves(inner)
    poly = product(q_high, t_high) + (product(q_high, t_low) + product(q_low, t_high))
    poly = poly + c1 * scaled + jnp.where(diagonal, c0, 0.0)
    return product(cube, poly.astype(jnp.bfloat16)).astype(jnp.bfloat16)


def kernel(plan, counts, coef_ref, x_ref, o_ref, cubes, done, sent, came, last):
    slot_0, cube_0, step_0 = grid(*plan[0])
    slot_1, cube_1, step_1 = grid(*plan[1])
    me = [lax.axis_index(axis) for axis in AXES]

    def device(step):
        return tuple(lax.rem(here + (s + n), n) for here, s, n in zip(me, step, counts))

    def part(ref, turn, cube, piece):
        return ref.at[turn, cube, pl.ds(pl.multiple_of(ROWS * piece, ROWS), ROWS)]

    def copy(stage, cube, piece):
        if stage == 0:
            source, target = x_ref.at[flat(slot_0(cube, piece))], part(cubes, 0, cube, piece)
            arrived, step = came.at[cube], step_0(cube, piece)
        elif stage == 1:
            after = cube_1(*slot_0(cube, piece))
            source, target = part(done, 0, cube, piece), part(cubes, 1, *after)
            arrived = came.at[4 + after[0]]
            step = minus(step_1(*after), step_0(cube, piece))
        else:
            source, target = part(done, 1, cube, piece), o_ref.at[flat(slot_1(cube, piece))]
            arrived, step = last, minus((0, 0, 0), step_1(cube, piece))
        return source, target, arrived, step

    def begin(stage, cube):
        def one(piece, carry):
            source, target, arrived, step = copy(stage, cube, piece)
            away = sum(s * s for s in step)
            if isinstance(away, int):
                pltpu.make_async_copy(source, target, arrived).start()
                return carry

            @pl.when(away > 0)
            def _():
                pltpu.make_async_remote_copy(
                    src_ref=source,
                    dst_ref=target,
                    send_sem=sent.at[stage],
                    recv_sem=arrived,
                    device_id=device(step),
                    device_id_type=pl.DeviceIdType.MESH,
                ).start()

            @pl.when(away == 0)
            def _():
                pltpu.make_async_copy(source, target, arrived).start()

            return carry

        lax.fori_loop(0, 8, one, 0)

    barrier = pltpu.get_barrier_semaphore()

    def greet(n, carry):
        @pl.when(n != 13)
        def _():
            pl.semaphore_signal(
                barrier,
                inc=1,
                device_id=device((n // 9 - 1, n // 3 % 3 - 1, n % 3 - 1)),
                device_id_type=pl.DeviceIdType.MESH,
            )

        return carry

    lax.fori_loop(0, 27, greet, 0)
    pl.semaphore_wait(barrier, 26)

    def enter(cube, carry):
        begin(0, cube)
        return carry

    lax.fori_loop(0, 4, enter, 0)
    coefficients = [coef_ref[n] for n in range(5)]
    diagonal = lax.broadcasted_iota(jnp.int32, (FRAMES, FRAMES), 0) == lax.broadcasted_iota(
        jnp.int32, (FRAMES, FRAMES), 1
    )

    def work(n, carry):
        turn, cube = n // 4, n % 4
        pltpu.make_async_copy(cubes.at[turn, cube], cubes.at[turn, cube], came.at[n]).wait()
        done[turn, cube] = shrink_cube(cubes[turn, cube], coefficients, diagonal)

        @pl.when(turn == 0)
        def _():
            begin(1, cube)

        @pl.when(turn == 1)
        def _():
            begin(2, cube)

        return carry

    lax.fori_loop(0, 8, work, 0)
    pltpu.make_async_copy(x_ref, o_ref, last).wait()
    away = [0, 0, 0]
    for n in range(32):
        for stage in range(3):
            away[stage] += any(copy_step(plan, stage, n // 8, n % 8))
    for stage in range(3):
        if away[stage]:
            some = pl.ds(0, away[stage])
            pltpu.make_async_copy(
                o_ref.at[some], o_ref.at[some], sent.at[stage]
            ).wait()


def copy_step(plan, stage, cube, piece):
    slot_0, _, step_0 = grid(*plan[0])
    _, cube_1, step_1 = grid(*plan[1])
    if stage == 0:
        return step_0(cube, piece)
    if stage == 1:
        return minus(step_1(*cube_1(*slot_0(cube, piece))), step_0(cube, piece))
    return step_1(cube, piece)


def denoise(pattern, counts, coefficients, pieces):
    kinds = (pattern // 9, pattern // 3 % 3, pattern % 3)
    plan = (
        ([kind != 1 for kind in kinds], OWNERS[pattern][0]),
        ([kind != 0 for kind in kinds], OWNERS[pattern][1]),
    )
    cubes = pltpu.VMEM((2, 4, CUBE, FRAMES), jnp.bfloat16)
    return pl.pallas_call(
        functools.partial(kernel, plan, counts),
        out_shape=jax.ShapeDtypeStruct(pieces.shape, pieces.dtype),
        in_specs=[
            pl.BlockSpec(memory_space=pltpu.SMEM),
            pl.BlockSpec(memory_space=pl.ANY),
        ],
        out_specs=pl.BlockSpec(memory_space=pl.ANY),
        scratch_shapes=[
            cubes, cubes,
            pltpu.SemaphoreType.DMA((3,)),
            pltpu.SemaphoreType.DMA((8,)),
            pltpu.SemaphoreType.DMA,
        ],
        compiler_params=pltpu.CompilerParams(
            collective_id=pattern, has_side_effects=True, vmem_limit_bytes=32 << 20
        ),
        name=f"denoise_{pattern}",
    )(coefficients, pieces)


def local(counts, volume, offsets, coefficients):
    sizes = volume.shape
    pieces = volume.reshape(4, 4, 4, 4, 2, 4, FRAMES).transpose(0, 2, 4, 1, 3, 5, 6)
    pieces = pieces.reshape(32, ROWS, FRAMES)
    kind = jnp.where(offsets[1] != 0, 1 + (offsets[0] != 0).astype(jnp.int32), 0)
    pattern = jnp.sum(kind * jnp.array([9, 3, 1], jnp.int32))
    branches = [functools.partial(denoise, n, counts) for n in range(27)]
    result = lax.switch(pattern, branches, coefficients, pieces)
    result = result.reshape(4, 4, 2, 4, 4, 4, FRAMES).transpose(0, 3, 1, 4, 2, 5, 6)
    return result.reshape(sizes)


def solution(mesh):
    counts = tuple(mesh.shape[axis] for axis in AXES)
    return jax.shard_map(
        functools.partial(local, counts),
        mesh=mesh,
        in_specs=(P("gx", "gy", "gz", None), P(), P()),
        out_specs=P("gx", "gy", "gz", None),
        check_vma=False,
    )
```

```python
import functools

import jax
import jax.numpy as jnp
from jax import lax
from jax.experimental import pallas as pl
from jax.experimental.pallas import tpu as pltpu
from jax.sharding import PartitionSpec as P

ROWS = 64
CUBE = 512
FRAMES = 256
AXES = ("gx", "gy", "gz")

OWNERS = [
    ((1, 3, 10), (0, 0, 0)), ((1, 2, 0), (0, 0, 3)), ((1, 3, 10), (0, 0, 12)),
    ((1, 0, 10), (0, 2, 0)), ((1, 0, 0), (0, 0, 5)), ((1, 0, 9), (0, 0, 12)),
    ((1, 3, 10), (0, 2, 0)), ((1, 2, 0), (0, 0, 5)), ((1, 3, 10), (0, 3, 10)),
    ((0, 0, 5), (1, 0, 0)), ((0, 1, 0), (2, 0, 5)), ((0, 0, 12), (1, 0, 9)),
    ((0, 0, 3), (1, 1, 0)), ((0, 0, 0), (1, 0, 5)), ((0, 0, 3), (1, 0, 5)),
    ((0, 0, 5), (1, 2, 0)), ((0, 1, 0), (1, 0, 5)), ((0, 0, 5), (1, 0, 5)),
    ((1, 3, 10), (2, 0, 0)), ((1, 2, 0), (2, 0, 3)), ((1, 2, 12), (2, 0, 12)),
    ((1, 0, 9), (1, 1, 0)), ((1, 0, 0), (1, 0, 5)), ((1, 0, 12), (1, 1, 12)),
    ((1, 2, 10), (1, 2, 0)), ((1, 2, 0), (1, 2, 3)), ((1, 3, 10), (1, 3, 10)),
]


def slot_of(moved, i, j, x, y, z):
    a = 2 * i + 1 + x * (1 - 4 * i) if moved[0] else 2 * i + x
    b = 2 * j + 1 + y * (1 - 4 * j) if moved[1] else 2 * j + y
    return 8 * a + 2 * b + (1 - z if moved[2] else z)


def regroup(before, after, i, x):
    if before == after:
        return i, x
    odd = i + x - 2 * i * x
    return (odd if before else 1 - odd), 1 - x


def step_of(moved, owners, i, j, x, y, z):
    x_bits = (owners[0] % 2, owners[0] // 2)
    y_bits = (owners[1] % 2, owners[1] // 2)
    bits = [owners[2] // 2**n % 2 for n in range(4)]
    step_x = i * (x_bits[0] + j * (x_bits[1] - x_bits[0]) - x) if moved[0] else 0
    step_y = j * (y_bits[0] + i * (y_bits[1] - y_bits[0]) - y) if moved[1] else 0
    step_z = 0
    if moved[2]:
        step_z = bits[0] + j * (bits[1] - bits[0]) + i * (bits[2] - bits[0])
        step_z = step_z + i * j * (bits[3] - bits[2] - bits[1] + bits[0]) - z
    return step_x, step_y, step_z


def move_of(plan, stage, i, j, x, y, z):
    (moved_0, owners_0), (moved_1, owners_1) = plan
    if stage == 0:
        return step_of(moved_0, owners_0, i, j, x, y, z)
    if stage == 2:
        return minus((0, 0, 0), step_of(moved_1, owners_1, i, j, x, y, z))
    return minus(
        step_of(moved_1, owners_1, *next_of(plan, i, j, x, y, z)),
        step_of(moved_0, owners_0, i, j, x, y, z),
    )


def next_of(plan, i, j, x, y, z):
    before, after = plan[0][0], plan[1][0]
    next_i, next_x = regroup(before[0], after[0], i, x)
    next_j, next_y = regroup(before[1], after[1], j, y)
    return next_i, next_j, next_x, next_y, (z if before[2] == after[2] else 1 - z)


def minus(left, right):
    return tuple(x - y for x, y in zip(left, right))


def shrink_cube(cube, coefficients, eye):
    c0, c1, c2, c3, c4 = coefficients

    def product(left, right, dims=((1,), (0,))):
        return lax.dot_general(
            left, right, (dims, ((), ())), preferred_element_type=jnp.float32
        )

    def halves(value):
        high = value.astype(jnp.bfloat16)
        return high, (value - high.astype(jnp.float32)).astype(jnp.bfloat16)

    def fine_product(left, right):
        return product(
            jnp.concatenate([left[0], left[0], left[1]], 1),
            jnp.concatenate([right[0], right[1], right[0]], 0),
        )

    gramian = product(cube, cube, ((0,), (0,)))
    trace = jnp.sum(gramian * eye, keepdims=True)
    scale = 1.0 / (CUBE * (trace / (CUBE * FRAMES) + 1e-6))
    scale_2 = scale * scale
    parts = halves(gramian)
    square = fine_product(parts, parts)
    inner = (c4 * scale_2) * square + (c3 * scale) * gramian
    poly = scale_2 * (fine_product(halves(inner), halves(square)) + c2 * square)
    poly = poly + ((c1 * scale) * gramian + c0 * eye)
    return product(cube, poly.astype(jnp.bfloat16)).astype(jnp.bfloat16)


def halve(even, odd):
    first = lax.broadcasted_iota(jnp.int32, even.shape, even.ndim - 2) < 4
    low = jnp.where(first, even, pltpu.roll(odd, 4, even.ndim - 2))
    return low, jnp.where(first, pltpu.roll(even, 4, even.ndim - 2), odd)


def kernel(
    plan, counts, coef_ref, x_ref, o_ref, raw, pieces, cubes, done, eye, coef, sent, came, last, own
):
    moves = [
        [move_of(plan, stage, *(n >> bit & 1 for bit in range(5))) for n in range(32)]
        for stage in range(3)
    ]
    peers = sorted({step for steps in moves for step in steps if any(step)})
    near = []
    for axis, count in zip(AXES, counts):
        here = lax.axis_index(axis)
        near.append((here, lax.rem(here + 1, count), lax.rem(here + (count - 1), count)))

    def device(step):
        where = []
        for (here, above, below), s in zip(near, step):
            if isinstance(s, int):
                where.append((here, above, below)[s])
            else:
                where.append(jnp.where(s > 0, above, jnp.where(s < 0, below, here)))
        return tuple(where)

    def part(turn, i, j, x, y, z):
        return turn, 2 * i + j, pl.ds(pl.multiple_of(ROWS * (4 * x + 2 * y + z), ROWS), ROWS)

    def begin(stage, i, j, x, y, z):
        if stage == 0:
            source = pieces.at[slot_of(plan[0][0], i, j, x, y, z)]
            target, arrived = cubes.at[part(0, i, j, x, y, z)], came.at[2 * i + j]
        elif stage == 1:
            after = next_of(plan, i, j, x, y, z)
            source, target = done.at[part(0, i, j, x, y, z)], cubes.at[part(1, *after)]
            arrived = came.at[4 + 2 * after[0] + after[1]]
        else:
            source = done.at[part(1, i, j, x, y, z)]
            target, arrived = o_ref.at[slot_of(plan[1][0], i, j, x, y, z)], last
        step = move_of(plan, stage, i, j, x, y, z)
        away = sum(s * s for s in step)
        if isinstance(away, int) and not away:
            pltpu.make_async_copy(source, target, arrived).start()
            return

        @pl.when(away > 0)
        def _():
            pltpu.make_async_remote_copy(
                src_ref=source,
                dst_ref=target,
                send_sem=sent.at[stage],
                recv_sem=arrived,
                device_id=device(step),
                device_id_type=pl.DeviceIdType.MESH,
            ).start()

        @pl.when(away == 0)
        def _():
            pltpu.make_async_copy(source, target, arrived).start()

    def begin_cube(stage, i, j):
        def plane(x, carry):
            def line(y, carry):
                begin(stage, i, j, x, y, 0)
                begin(stage, i, j, x, y, 1)
                return carry

            return lax.fori_loop(0, 2, line, carry)

        lax.fori_loop(0, 2, plane, 0)

    def every_cube(action):
        def outer(i, carry):
            def inner(j, carry):
                action(i, j)
                return carry

            return lax.fori_loop(0, 2, inner, carry)

        lax.fori_loop(0, 2, outer, 0)

    load = pltpu.make_async_copy(x_ref, raw, own.at[0])
    load.start()
    fetch = pltpu.make_async_copy(coef_ref, coef, own.at[1])
    fetch.start()
    barrier = pltpu.get_barrier_semaphore()
    for step in peers:
        pl.semaphore_signal(
            barrier,
            inc=1,
            device_id=device(minus((0, 0, 0), step)),
            device_id_type=pl.DeviceIdType.MESH,
        )
    load.wait()
    fetch.wait()

    def cut(a, carry):
        def row(b, carry):
            def some(x, carry):
                block = raw[pl.ds(4 * a + 2 * x, 2), pl.ds(4 * b, 4)]
                pairs = block.astype(jnp.float32).reshape(4, 2, 8, FRAMES)
                for c, half in enumerate(halve(pairs[:, 0], pairs[:, 1])):
                    rows = pl.ds(pl.multiple_of(32 * x, 32), 32)
                    half = half.reshape(32, FRAMES).astype(jnp.bfloat16)
                    pieces[8 * a + 2 * b + c, rows] = half
                return carry

            return lax.fori_loop(0, 2, some, carry)

        return lax.fori_loop(0, 4, row, carry)

    lax.fori_loop(0, 4, cut, 0)
    pl.semaphore_wait(barrier, len(peers))
    every_cube(functools.partial(begin_cube, 0))
    coefficients = [coef[n] for n in range(5)]
    eye[...] = (
        lax.broadcasted_iota(jnp.int32, (FRAMES, FRAMES), 0)
        == lax.broadcasted_iota(jnp.int32, (FRAMES, FRAMES), 1)
    ).astype(jnp.float32)

    def one_pass(turn, carry):
        def work(i, j):
            cube = 2 * i + j
            here = cubes.at[turn, cube]
            pltpu.make_async_copy(here, here, came.at[4 * turn + cube]).wait()
            done[turn, cube] = shrink_cube(cubes[turn, cube], coefficients, eye[...])

            @pl.when(turn == 0)
            def _():
                begin_cube(1, i, j)

            @pl.when(turn == 1)
            def _():
                begin_cube(2, i, j)

        every_cube(work)
        return carry

    lax.fori_loop(0, 2, one_pass, 0)
    pltpu.make_async_copy(o_ref, o_ref, last).wait()
    for stage in range(3):
        count = sum(any(step) for step in moves[stage])
        if count:
            some = o_ref.at[pl.ds(0, count)]
            pltpu.make_async_copy(some, some, sent.at[stage]).wait()


def denoise(pattern, counts, coefficients, volume):
    kinds = (pattern // 9, pattern // 3 % 3, pattern % 3)
    plan = (
        ([kind != 1 for kind in kinds], OWNERS[pattern][0]),
        ([kind != 0 for kind in kinds], OWNERS[pattern][1]),
    )
    pieces = (32, ROWS, FRAMES)
    cubes = pltpu.VMEM((2, 4, CUBE, FRAMES), jnp.bfloat16)
    return pl.pallas_call(
        functools.partial(kernel, plan, counts),
        out_shape=jax.ShapeDtypeStruct(pieces, jnp.bfloat16),
        in_specs=[
            pl.BlockSpec(memory_space=pl.ANY),
            pl.BlockSpec(memory_space=pl.ANY),
        ],
        out_specs=pl.BlockSpec(memory_space=pl.ANY),
        scratch_shapes=[
            pltpu.VMEM(volume.shape, jnp.bfloat16),
            pltpu.VMEM(pieces, jnp.bfloat16),
            cubes, cubes,
            pltpu.VMEM((FRAMES, FRAMES), jnp.float32),
            pltpu.SMEM((5,), jnp.float32),
            pltpu.SemaphoreType.DMA((3,)),
            pltpu.SemaphoreType.DMA((8,)),
            pltpu.SemaphoreType.DMA,
            pltpu.SemaphoreType.DMA((2,)),
        ],
        compiler_params=pltpu.CompilerParams(
            collective_id=pattern, has_side_effects=True, vmem_limit_bytes=32 << 20
        ),
        name=f"denoise_{pattern}",
    )(coefficients, volume)


def pattern_kernel(offsets, pattern):
    total = 0
    for dim in range(3):
        early = (offsets[0, dim] != 0).astype(jnp.int32)
        late = (offsets[1, dim] != 0).astype(jnp.int32)
        total = 3 * total + late * (1 + early)
    pattern[0] = total


def join_kernel(pieces, volume):
    for b in range(4):
        low, high = (
            pieces[2 * b + c].astype(jnp.float32).reshape(8, 8, FRAMES) for c in range(2)
        )
        first = lax.broadcasted_iota(jnp.int32, low.shape, 1) < 4
        even = jnp.where(first, low, pltpu.roll(high, 4, 1)).astype(jnp.bfloat16)
        odd = jnp.where(first, pltpu.roll(low, 4, 1), high).astype(jnp.bfloat16)
        for x in range(4):
            for y in range(2):
                volume[x, 4 * b + 2 * y] = even[2 * x + y]
                volume[x, 4 * b + 2 * y + 1] = odd[2 * x + y]


def local(counts, volume, offsets, coefficients):
    pattern = pl.pallas_call(
        pattern_kernel,
        out_shape=jax.ShapeDtypeStruct((1,), jnp.int32),
        in_specs=[pl.BlockSpec(memory_space=pltpu.SMEM)],
        out_specs=pl.BlockSpec(memory_space=pltpu.SMEM),
        name="pattern",
    )(offsets)[0]
    branches = [functools.partial(denoise, n, counts) for n in range(27)]
    pieces = lax.switch(pattern, branches, coefficients, volume)
    sizes = volume.shape
    return pl.pallas_call(
        join_kernel,
        out_shape=jax.ShapeDtypeStruct(sizes, volume.dtype),
        grid=(4,),
        in_specs=[pl.BlockSpec((8, ROWS, FRAMES), lambda a: (a, 0, 0))],
        out_specs=pl.BlockSpec((4, *sizes[1:]), lambda a: (a, 0, 0, 0)),
        name="join",
    )(pieces)


def solution(mesh):
    counts = tuple(mesh.shape[axis] for axis in AXES)
    return jax.shard_map(
        functools.partial(local, counts),
        mesh=mesh,
        in_specs=(P("gx", "gy", "gz", None), P(), P()),
        out_specs=P("gx", "gy", "gz", None),
        check_vma=False,
    )
```

```python
import functools

import jax
import jax.numpy as jnp
from jax import lax
from jax.experimental import pallas as pl
from jax.experimental.pallas import tpu as pltpu
from jax.sharding import PartitionSpec as P

ROWS = 64
CUBE = 512
FRAMES = 256
AXES = ("gx", "gy", "gz")

OWNERS = [
    ((1, 3, 10), (0, 0, 0)), ((1, 2, 0), (0, 0, 3)), ((1, 3, 10), (0, 0, 12)),
    ((1, 0, 10), (0, 2, 0)), ((1, 0, 0), (0, 0, 5)), ((1, 0, 9), (0, 0, 12)),
    ((1, 3, 10), (0, 2, 0)), ((1, 2, 0), (0, 0, 5)), ((1, 3, 10), (0, 3, 10)),
    ((0, 0, 5), (1, 0, 0)), ((0, 1, 0), (2, 0, 5)), ((0, 0, 12), (1, 0, 9)),
    ((0, 0, 3), (1, 1, 0)), ((0, 0, 0), (1, 0, 5)), ((0, 0, 3), (1, 0, 5)),
    ((0, 0, 5), (1, 2, 0)), ((0, 1, 0), (1, 0, 5)), ((0, 0, 5), (1, 0, 5)),
    ((1, 3, 10), (2, 0, 0)), ((1, 2, 0), (2, 0, 3)), ((1, 2, 12), (2, 0, 12)),
    ((1, 0, 9), (1, 1, 0)), ((1, 0, 0), (1, 0, 5)), ((1, 0, 12), (1, 1, 12)),
    ((1, 2, 10), (1, 2, 0)), ((1, 2, 0), (1, 2, 3)), ((1, 3, 10), (1, 3, 10)),
]


def slot_of(moved, i, j, x, y, z):
    a = 2 * i + 1 + x * (1 - 4 * i) if moved[0] else 2 * i + x
    b = 2 * j + 1 + y * (1 - 4 * j) if moved[1] else 2 * j + y
    return a, b, 1 - z if moved[2] else z


def number(slot):
    return 8 * slot[0] + 2 * slot[1] + slot[2]


def regroup(before, after, i, x):
    if before == after:
        return i, x
    odd = i + x - 2 * i * x
    return (odd if before else 1 - odd), 1 - x


def step_of(moved, owners, i, j, x, y, z):
    x_bits = (owners[0] % 2, owners[0] // 2)
    y_bits = (owners[1] % 2, owners[1] // 2)
    bits = [owners[2] // 2**n % 2 for n in range(4)]
    step_x = i * (x_bits[0] + j * (x_bits[1] - x_bits[0]) - x) if moved[0] else 0
    step_y = j * (y_bits[0] + i * (y_bits[1] - y_bits[0]) - y) if moved[1] else 0
    step_z = 0
    if moved[2]:
        step_z = bits[0] + j * (bits[1] - bits[0]) + i * (bits[2] - bits[0])
        step_z = step_z + i * j * (bits[3] - bits[2] - bits[1] + bits[0]) - z
    return step_x, step_y, step_z


def move_of(plan, stage, i, j, x, y, z):
    (moved_0, owners_0), (moved_1, owners_1) = plan
    if stage == 0:
        return step_of(moved_0, owners_0, i, j, x, y, z)
    if stage == 2:
        return minus((0, 0, 0), step_of(moved_1, owners_1, i, j, x, y, z))
    return minus(
        step_of(moved_1, owners_1, *next_of(plan, i, j, x, y, z)),
        step_of(moved_0, owners_0, i, j, x, y, z),
    )


def next_of(plan, i, j, x, y, z):
    before, after = plan[0][0], plan[1][0]
    next_i, next_x = regroup(before[0], after[0], i, x)
    next_j, next_y = regroup(before[1], after[1], j, y)
    return next_i, next_j, next_x, next_y, (z if before[2] == after[2] else 1 - z)


def minus(left, right):
    return tuple(x - y for x, y in zip(left, right))


def shrink_cube(cube, coefficients, eye):
    c0, c1, c2, c3, c4 = coefficients

    def product(left, right, dims=((1,), (0,))):
        return lax.dot_general(
            left, right, (dims, ((), ())), preferred_element_type=jnp.float32
        )

    def halves(value):
        high = value.astype(jnp.bfloat16)
        return high, (value - high.astype(jnp.float32)).astype(jnp.bfloat16)

    def fine_product(left, right):
        return product(
            jnp.concatenate([left[0], left[0], left[1]], 1),
            jnp.concatenate([right[0], right[1], right[0]], 0),
        )

    gramian = product(cube, cube, ((0,), (0,)))
    trace = jnp.sum(gramian * eye, keepdims=True)
    scale = 1.0 / (CUBE * (trace / (CUBE * FRAMES) + 1e-6))
    scale_2 = scale * scale
    parts = halves(gramian)
    square = fine_product(parts, parts)
    inner = (c4 * scale_2) * square + (c3 * scale) * gramian
    poly = scale_2 * (fine_product(halves(inner), halves(square)) + c2 * square)
    poly = poly + ((c1 * scale) * gramian + c0 * eye)
    return product(cube, poly.astype(jnp.bfloat16)).astype(jnp.bfloat16)


def halve(even, odd):
    first = lax.broadcasted_iota(jnp.int32, even.shape, even.ndim - 2) < 4
    low = jnp.where(first, even, pltpu.roll(odd, 4, even.ndim - 2))
    return low, jnp.where(first, pltpu.roll(even, 4, even.ndim - 2), odd)


def kernel(
    plan, flips, counts, coef_ref, x_ref, o_ref, raw, pieces, cubes, done, eye, coef, sent, came, last, own
):
    moves = [
        [move_of(plan, stage, *(n >> bit & 1 for bit in range(5))) for n in range(32)]
        for stage in range(3)
    ]
    peers = sorted({step for steps in moves for step in steps if any(step)})
    near = []
    for axis, count in zip(AXES, counts):
        here = lax.axis_index(axis)
        near.append((here, lax.rem(here + 1, count), lax.rem(here + (count - 1), count)))

    def device(step):
        where = []
        for (here, above, below), s in zip(near, step):
            if isinstance(s, int):
                where.append((here, above, below)[s])
            else:
                where.append(jnp.where(s > 0, above, jnp.where(s < 0, below, here)))
        return tuple(where)

    def part(turn, i, j, x, y, z):
        return turn, 2 * i + j, pl.ds(pl.multiple_of(ROWS * (4 * x + 2 * y + z), ROWS), ROWS)

    def begin(stage, i, j, x, y, z):
        if stage == 0:
            source = pieces.at[number(slot_of(plan[0][0], i, j, x, y, z))]
            target, arrived = cubes.at[part(0, i, j, x, y, z)], came.at[2 * i + j]
        elif stage == 1:
            after = next_of(plan, i, j, x, y, z)
            source, target = done.at[part(0, i, j, x, y, z)], cubes.at[part(1, *after)]
            arrived = came.at[4 + 2 * after[0] + after[1]]
        else:
            source = done.at[part(1, i, j, x, y, z)]
            target, arrived = o_ref.at[number(slot_of(plan[1][0], i, j, x, y, z))], last
        step = move_of(plan, stage, i, j, x, y, z)
        away = sum(s * s for s in step)
        if isinstance(away, int) and not away:
            pltpu.make_async_copy(source, target, arrived).start()
            return

        @pl.when(away > 0)
        def _():
            pltpu.make_async_remote_copy(
                src_ref=source,
                dst_ref=target,
                send_sem=sent.at[stage],
                recv_sem=arrived,
                device_id=device(step),
                device_id_type=pl.DeviceIdType.MESH,
            ).start()

        @pl.when(away == 0)
        def _():
            pltpu.make_async_copy(source, target, arrived).start()

    def cut(slot_a, slot_b):
        block = raw[pl.ds(4 * slot_a, 4), pl.ds(4 * slot_b, 4)]
        pairs = block.astype(jnp.float32).reshape(8, 2, 8, FRAMES)
        for c, half in enumerate(halve(pairs[:, 0], pairs[:, 1])):
            half = half.reshape(ROWS, FRAMES).astype(jnp.bfloat16)
            pieces[8 * slot_a + 2 * slot_b + c] = half

    def begin_cube(stage, i, j):
        def plane(x, carry):
            def line(y, carry):
                if stage == 0:
                    cut(*slot_of(plan[0][0], i, j, x, y, 0)[:2])
                begin(stage, i, j, x, y, 0)
                begin(stage, i, j, x, y, 1)
                return carry

            return lax.fori_loop(0, 2, line, carry)

        lax.fori_loop(0, 2, plane, 0)

    def every_cube(action):
        def outer(i, carry):
            def inner(j, carry):
                action(i, j)
                return carry

            return lax.fori_loop(0, 2, inner, carry)

        lax.fori_loop(0, 2, outer, 0)

    load = pltpu.make_async_copy(x_ref, raw, own.at[0])
    load.start()
    fetch = pltpu.make_async_copy(coef_ref, coef, own.at[1])
    fetch.start()
    barrier = pltpu.get_barrier_semaphore()
    for step in peers:
        pl.semaphore_signal(
            barrier,
            inc=1,
            device_id=device(minus((0, 0, 0), step)),
            device_id_type=pl.DeviceIdType.MESH,
        )
    load.wait()
    fetch.wait()

    pl.semaphore_wait(barrier, len(peers))
    every_cube(functools.partial(begin_cube, 0))
    coefficients = [coef[n] for n in range(5)]
    eye[...] = (
        lax.broadcasted_iota(jnp.int32, (FRAMES, FRAMES), 0)
        == lax.broadcasted_iota(jnp.int32, (FRAMES, FRAMES), 1)
    ).astype(jnp.float32)

    def one_pass(turn, carry):
        def work(i, j):
            if flips[0]:
                i = i + turn * (1 - 2 * i)
            if flips[1]:
                j = j + turn * (1 - 2 * j)
            cube = 2 * i + j
            here = cubes.at[turn, cube]
            pltpu.make_async_copy(here, here, came.at[4 * turn + cube]).wait()
            done[turn, cube] = shrink_cube(cubes[turn, cube], coefficients, eye[...])

            @pl.when(turn == 0)
            def _():
                begin_cube(1, i, j)

            @pl.when(turn == 1)
            def _():
                begin_cube(2, i, j)

        every_cube(work)
        return carry

    lax.fori_loop(0, 2, one_pass, 0)
    pltpu.make_async_copy(o_ref, o_ref, last).wait()
    for stage in range(3):
        count = sum(any(step) for step in moves[stage])
        if count:
            some = o_ref.at[pl.ds(0, count)]
            pltpu.make_async_copy(some, some, sent.at[stage]).wait()


def denoise(pattern, counts, coefficients, volume):
    kinds = (pattern // 9, pattern // 3 % 3, pattern % 3)
    plan = (
        ([kind != 1 for kind in kinds], OWNERS[pattern][0]),
        ([kind != 0 for kind in kinds], OWNERS[pattern][1]),
    )
    flips = [kind == 1 or kinds == (2, 2, 2) for kind in kinds[:2]]
    pieces = (32, ROWS, FRAMES)
    cubes = pltpu.VMEM((2, 4, CUBE, FRAMES), jnp.bfloat16)
    return pl.pallas_call(
        functools.partial(kernel, plan, flips, counts),
        out_shape=jax.ShapeDtypeStruct(pieces, jnp.bfloat16),
        in_specs=[
            pl.BlockSpec(memory_space=pltpu.HBM),
            pl.BlockSpec(memory_space=pl.ANY),
        ],
        out_specs=pl.BlockSpec(memory_space=pl.ANY),
        scratch_shapes=[
            pltpu.VMEM(volume.shape, jnp.bfloat16),
            pltpu.VMEM(pieces, jnp.bfloat16),
            cubes, cubes,
            pltpu.VMEM((FRAMES, FRAMES), jnp.float32),
            pltpu.SMEM((5,), jnp.float32),
            pltpu.SemaphoreType.DMA((3,)),
            pltpu.SemaphoreType.DMA((8,)),
            pltpu.SemaphoreType.DMA,
            pltpu.SemaphoreType.DMA((2,)),
        ],
        compiler_params=pltpu.CompilerParams(
            collective_id=pattern, has_side_effects=True, vmem_limit_bytes=32 << 20
        ),
        name=f"denoise_{pattern}",
    )(coefficients, volume)


def pattern_kernel(offsets, pattern):
    total = 0
    for dim in range(3):
        early = (offsets[0, dim] != 0).astype(jnp.int32)
        late = (offsets[1, dim] != 0).astype(jnp.int32)
        total = 3 * total + late * (1 + early)
    pattern[0] = total


def join_kernel(pieces, volume):
    for a, b in [(a, b) for a in range(2) for b in range(4)]:
        low, high = (
            pieces[8 * a + 2 * b + c].astype(jnp.float32).reshape(8, 8, FRAMES)
            for c in range(2)
        )
        first = lax.broadcasted_iota(jnp.int32, low.shape, 1) < 4
        even = jnp.where(first, low, pltpu.roll(high, 4, 1)).astype(jnp.bfloat16)
        odd = jnp.where(first, pltpu.roll(low, 4, 1), high).astype(jnp.bfloat16)
        for x in range(4):
            for y in range(2):
                volume[4 * a + x, 4 * b + 2 * y] = even[2 * x + y]
                volume[4 * a + x, 4 * b + 2 * y + 1] = odd[2 * x + y]


def local(counts, volume, offsets, coefficients):
    pattern = pl.pallas_call(
        pattern_kernel,
        out_shape=jax.ShapeDtypeStruct((1,), jnp.int32),
        in_specs=[pl.BlockSpec(memory_space=pltpu.SMEM)],
        out_specs=pl.BlockSpec(memory_space=pltpu.SMEM),
        name="pattern",
    )(offsets)[0]
    branches = [functools.partial(denoise, n, counts) for n in range(27)]
    pieces = lax.switch(pattern, branches, coefficients, volume)
    sizes = volume.shape
    return pl.pallas_call(
        join_kernel,
        out_shape=jax.ShapeDtypeStruct(sizes, volume.dtype),
        grid=(2,),
        in_specs=[pl.BlockSpec((16, ROWS, FRAMES), lambda a: (a, 0, 0))],
        out_specs=pl.BlockSpec((8, *sizes[1:]), lambda a: (a, 0, 0, 0)),
        name="join",
    )(pieces)


def solution(mesh):
    counts = tuple(mesh.shape[axis] for axis in AXES)
    return jax.shard_map(
        functools.partial(local, counts),
        mesh=mesh,
        in_specs=(P("gx", "gy", "gz", None), P(), P()),
        out_specs=P("gx", "gy", "gz", None),
        check_vma=False,
    )
```
